256 devices in a mesh: member: 16 (over y, x_hi, core), domain: 16 (over x_lo, z).
Axes of the slice: x: 4 (x_hi: 2, x_lo: 2; x = x_hi * 2 + x_lo), y: 4, z: 8, core: 2. Of those that a mesh axis runs over, the one named last changes fastest.
Arguments:
- state: float32 [16, 4, 512, 512], P('member', None, 'domain'), may hold values from -5 to 5
- perturbation: float32 [16, 4, 512, 512], P('member', None, 'domain'), may hold values from -3 to 3
- parents: int32 [16], replicated, may hold values from 0 to 15
Outputs:
- final_state: float32 [16, 4, 512, 512], P('member', None, 'domain')
- score: float32 [16], P('member')
The draws below stay inside these ranges and needn't reach their ends.
Inputs may be any that keep to these rules, and one draw needn't show every extreme that they name: `parents`: A member may be the parent of several slots or of none.
All inputs are finite; a program needn't handle non-finite values.
Results may differ from the reference program's by a relative error of at most 0.00002.
Values sent between devices are 32-bit elements; how exact they have to be, the bound alone decides.
A program may use at most 64 MiB of HBM per device.

```python
import math
import jax
import jax.numpy as jnp
import numpy as np
from jax import lax

NLON = 512
STEPS = 3
MEMBERS = 16
NLAT = 512


def set_ends(drawn, own_key, smallest, top_value):
    longest = drawn.shape.index(max(drawn.shape))
    spots = []
    for shift in (0, 1):
        where = [jax.random.randint(jax.random.fold_in(own_key, axis), (), 0, length) for axis, length in enumerate(drawn.shape)]
        where[longest] = (where[longest] + shift) % drawn.shape[longest]
        spots.append(tuple(where))
    return drawn.at[spots[0]].set(smallest).at[spots[1]].set(top_value)


def level_of(key, shape, shards, least, high):
    gain, own = 1.0, jax.random.fold_in(key, 6)
    for axis_at, parts in shards:
        steps = jnp.exp(jax.random.uniform(jax.random.fold_in(own, axis_at), (parts,), jnp.float32, least / len(shards), high / len(shards)))
        gain = gain * jnp.repeat(steps, shape[axis_at] // parts).reshape([-1 if axis == axis_at else 1 for axis in range(len(shape))])
    return gain


def rank_bounds(number_of, skew):
    portions = [(1 << 20) // math.isqrt(standing ** skew) + 1 for standing in range(1, number_of + 1)]
    deviation = 1 + sum(portions) // (1 << 30)
    return np.cumsum(np.array([max(1, weight // deviation) for weight in portions]))


def ranked_ids(stream_key, shape, count, lean):
    grid = rank_bounds(count, lean)
    pick = jax.random.randint(jax.random.fold_in(stream_key, 1), shape, 0, int(grid[count - 1]))
    grade = jnp.searchsorted(jnp.asarray(grid, jnp.int32), pick, side="right")
    return jax.random.permutation(jax.random.fold_in(stream_key, 2), count)[grade].astype(jnp.int32)


def noise(key, shape, deviation, bound, shards=(), kind=jnp.bfloat16):
    result = jax.random.normal(key, shape, jnp.float32) * deviation
    if len(shards) > 0:
        result = level_of(key, shape, shards, -0.22, 0.18) * result
    return jnp.clip(result, min=-bound, max=bound).astype(kind)


def setup_inputs(seed: int = 0) -> dict:
    streams_of = jax.random.split(jax.random.key(seed), 4)
    state = noise(streams_of[0], (MEMBERS, 4, NLAT, NLON), 0.5, 5.0, ((0, 16), (2, 16)), jnp.float32)
    perturbation = noise(streams_of[1], (MEMBERS, 4, NLAT, NLON), 0.3, 3.0, ((0, 16), (2, 16)), jnp.float32)
    parents = set_ends(ranked_ids(streams_of[2], (MEMBERS,), MEMBERS, 2), jax.random.fold_in(streams_of[2], 3), 0, MEMBERS - 1).astype(jnp.int32)
    return dict(state=state, perturbation=perturbation, parents=parents)


time_step = 0.1
viscous = 0.05
coriolis = 1.0


def gradients(padded):
    middle = padded[:, 1:-1]
    east = jnp.roll(middle, -1, axis=-1)
    west = jnp.roll(middle, 1, axis=-1)
    return middle, east, west, padded[:, 2:], padded[:, :-2]


def tendency(padded, start_row, total_rows):
    middle, east, west, north, south = gradients(padded)
    grad_x = (east - west) * 0.5
    grad_y = (north - south) * 0.5
    laplace = east + west + north + south - 4.0 * middle
    depth = 1.0 + padded[0]
    fluxes = jnp.stack([depth * padded[1], depth * padded[2]])
    flux_mid, flux_east, flux_west, flux_north, flux_south = gradients(fluxes)
    count = padded.shape[1] - 2
    global_rows = (start_row + 1 + jnp.arange(count, dtype=jnp.int32)).astype(jnp.float32)
    latitude = coriolis * (2.0 * (global_rows + 0.5) / total_rows - 1.0)
    latitude = latitude[:, None]
    height, speed_u, speed_v, tracer = middle[0], middle[1], middle[2], middle[3]
    advect = speed_u * grad_x + speed_v * grad_y
    d_eta = -((flux_east[0] - flux_west[0]) * 0.5 + (flux_north[1] - flux_south[1]) * 0.5) + viscous * laplace[0]
    d_u = -advect[1] + latitude * speed_v - grad_x[0] + viscous * laplace[1]
    d_v = -advect[2] - latitude * speed_u - grad_y[0] + viscous * laplace[2]
    d_q = -advect[3] + viscous * laplace[3]
    return jnp.stack([d_eta, d_u, d_v, d_q])


def operator(field):
    return tendency(jnp.pad(field, ((0, 0), (1, 1), (0, 0))), -1, NLAT)


def rk_step(field):
    first = field + time_step * operator(field)
    second = 0.75 * field + 0.25 * (first + time_step * operator(first))
    return (1.0 / 3.0) * field + (2.0 / 3.0) * (second + time_step * operator(second))


def run_steps(field):
    for count in range(STEPS):
        field = rk_step(field)
    return field


def reference(state, perturbation, parents):
    before = lax.map(run_steps, state)
    weight = 1.0 + 2.0 * jnp.arange(NLAT, dtype=jnp.int32).astype(jnp.float32) / (NLAT - 1)
    score = jnp.sum(weight[None, :, None] * before[:, 3] * before[:, 3], axis=(1, 2)) / (NLAT * NLON)
    cloned = jnp.take(before, parents, axis=0) + perturbation
    after = lax.map(run_steps, cloned)
    return after, score
```

```python
import jax
import jax.numpy as jnp
from jax import lax
from jax.experimental import pallas as pl
from jax.experimental.pallas import tpu as pltpu
from jax.sharding import PartitionSpec as P

F32 = jnp.float32
MESH = pl.DeviceIdType.MESH
STEPS = 3
STAGES = 3 * STEPS
time_step = 0.1
viscous = 0.05
coriolis = 1.0

FIELDS, CHUNKS, LANES = 4, 4, 128
OWN = 16
BUFFER_ROWS = 64
HALO = STAGES
PIECES = ((0, 16), (16, 16))


def stage(src, base, dst, start, groups, weight, old, lat0, lat1):
    lane = lax.broadcasted_iota(jnp.int32, (8, LANES), 1)
    row = lax.broadcasted_iota(jnp.int32, (8, LANES), 0).astype(F32)
    last, first = lane == LANES - 1, lane == 0
    keep = weight * (1.0 - 4.0 * viscous * time_step)
    spread = weight * viscous * time_step
    half = -weight * time_step * 0.5
    turn = weight * time_step * coriolis

    def body(group, carry):
        r = start + 8 * group
        here, north, south = pl.ds(r, 8), pl.ds(r + 1, 8), pl.ds(r - 1, 8)
        lat = ((row + r.astype(F32)) * lat1 + lat0) * turn
        cells = [[src[f, c, here, :] for c in range(CHUNKS)] for f in range(FIELDS)]
        to_west = [[pltpu.roll(cells[f][c], LANES - 1, 1) for c in range(CHUNKS)] for f in range(FIELDS)]
        to_east = [[pltpu.roll(cells[f][c], 1, 1) for c in range(CHUNKS)] for f in range(FIELDS)]
        for c in range(CHUNKS):
            E, W, N, S, dx, dy, out = [], [], [], [], [], [], []
            for f in range(FIELDS):
                e = jnp.where(last, to_west[f][(c + 1) % CHUNKS], to_west[f][c])
                w = jnp.where(first, to_east[f][(c - 1) % CHUNKS], to_east[f][c])
                n, s = src[f, c, north, :], src[f, c, south, :]
                E.append(e)
                W.append(w)
                N.append(n)
                S.append(s)
                dx.append(e - w)
                dy.append(n - s)
                o = keep * cells[f][c] + spread * ((e + w) + (n + s))
                if base is not None:
                    o = o + old * base[f, c, here, :]
                out.append(o)
            u, v = cells[1][c], cells[2][c]
            us, vs = half * u, half * v
            flux = (E[0] * E[1] - W[0] * W[1]) + (N[0] * N[2] - S[0] * S[2]) + (dx[1] + dy[2])
            dst[0, c, here, :] = out[0] + half * flux
            dst[1, c, here, :] = out[1] + (us * dx[1] + vs * dy[1]) + (lat * v + half * dx[0])
            dst[2, c, here, :] = out[2] + (us * dx[2] + vs * dy[2]) + (half * dy[0] - lat * u)
            dst[3, c, here, :] = out[3] + (us * dx[3] + vs * dy[3])
        return carry

    lax.fori_loop(0, groups, body, 0)


def kernel(
    parents, state, perturbation, after, score,
    A, C, S1, S2, noise, acc, got, *rest,
):
    pieces = len(PIECES)
    H, V, Q, X, T, U = (rest[i * pieces:(i + 1) * pieces] for i in range(6))
    (load_sem, halo_send, halo_recv, sum_send, sum_recv, out_sem,
     y_send, y_recv, x_send, x_recv, swap_send, swap_recv) = rest[6 * pieces:]
    m, d = lax.axis_index("member"), lax.axis_index("domain")
    y, xh, core = m // 4, (m // 2) % 2, m % 2
    xl, z = d // 8, d % 8
    rows = state.shape[2]
    domains = 16
    total_rows = rows * domains

    def member(y_, xh_, core_):
        return (y_ * 2 + xh_) * 2 + core_

    y_next, y_prev = (y + 1) % 4, (y + 3) % 4
    x_next = (member(y, (xh + xl) % 2, core), (1 - xl) * 8 + z)
    x_prev = (member(y, (xh + 1 - xl) % 2, core), (1 - xl) * 8 + z)
    other = (member(y, xh, 1 - core), d)
    d_next, d_prev = (m, (d + 1) % domains), (m, (d + domains - 1) % domains)

    def flip(size):
        return (m, d + size - 2 * size * ((d // size) % 2))

    sizes = (1, 2, 4, 8)
    greeted = [d_next, d_prev, x_next, x_prev, other] + [flip(s) for s in sizes]
    greeted += [(member(yy, xh, k), d) for yy in (y_next, y_prev) for k in (0, 1)]

    loads = []
    for c in range(CHUNKS):
        lanes = pl.ds(c * LANES, LANES)
        loads.append(pltpu.make_async_copy(state.at[0, :, :, lanes], A.at[:, c, pl.ds(OWN, rows), :], load_sem.at[0, c]))
    for c in range(CHUNKS):
        lanes = pl.ds(c * LANES, LANES)
        loads.append(pltpu.make_async_copy(perturbation.at[0, :, :, lanes], noise.at[:, c, :, :], load_sem.at[1, c]))
    for load in loads:
        load.start()

    barrier = pltpu.get_barrier_semaphore()
    for device in greeted:
        pl.semaphore_signal(barrier, inc=1, device_id=device, device_id_type=MESH)
    pl.semaphore_wait(barrier, len(greeted))

    def remote(src, dst, send, recv, device):
        copy = pltpu.make_async_remote_copy(
            src_ref=src, dst_ref=dst, send_sem=send, recv_sem=recv, device_id=device, device_id_type=MESH
        )
        copy.start()
        return copy

    def exchange(B, which):
        south = remote(B.at[:, :, pl.ds(OWN, HALO), :], B.at[:, :, pl.ds(OWN + rows, HALO), :],
                       halo_send.at[which, 0], halo_recv.at[which, 0], d_prev)
        north = remote(B.at[:, :, pl.ds(OWN + rows - HALO, HALO), :], B.at[:, :, pl.ds(OWN - HALO, HALO), :],
                       halo_send.at[which, 1], halo_recv.at[which, 1], d_next)
        south.wait()
        north.wait()

    nothing = jnp.zeros((FIELDS, CHUNKS, 8, LANES), F32)

    def clear_ends(B):
        @pl.when(d == 0)
        def _():
            B[:, :, pl.ds(OWN - 8, 8), :] = nothing

        @pl.when(d == domains - 1)
        def _():
            B[:, :, pl.ds(OWN + rows, 8), :] = nothing

    first_row = (d * rows - OWN).astype(F32)
    lat0 = 2.0 * (first_row + 0.5) / total_rows - 1.0
    lat1 = 2.0 / total_rows

    def run_steps(B):
        clear_ends(B)
        for k in range(1, STAGES + 1):
            groups = -(-(rows + 2 * (STAGES - k)) // 8)
            src, base, dst, weight, old = (
                (B, None, S1, 1.0, 0.0), (S1, B, S2, 0.25, 0.75), (S2, B, B, 2.0 / 3.0, 1.0 / 3.0)
            )[(k - 1) % 3]
            stage(src, base, dst, OWN - STAGES + k, groups, weight, old, lat0, lat1)
            if k < STAGES:
                clear_ends(dst)

    for load in loads:
        load.wait()
    exchange(A, 0)
    run_steps(A)

    pending = []
    mine, theirs = pl.ds(2 * core, 2), pl.ds(2 * (1 - core), 2)
    ring = []
    for i, (begin, count) in enumerate(PIECES):
        part = pl.ds(OWN + begin, count)
        place = H[i].at[y, core]
        local = pltpu.make_async_copy(A.at[mine, :, part, :], place, y_send.at[i, 7])
        local.start()
        copies = [local]
        for way, yy in enumerate((y_next, y_prev)):
            for k in (0, 1):
                copies.append(remote(A.at[pl.ds(2 * k, 2), :, part, :], place, y_send.at[i, 2 * way + k],
                                     y_recv.at[i, way, core], (member(yy, xh, k), d)))
        swap = remote(A.at[theirs, :, part, :], place, y_send.at[i, 4], y_recv.at[i, 2, 0], other)
        copies.append(swap)
        ring.append(copies)

    weight_row = lax.broadcasted_iota(jnp.int32, (8, LANES), 0).astype(F32)
    total = jnp.zeros((8, LANES), F32)
    for g in range(rows // 8):
        w = 1.0 + 2.0 * (weight_row + (d * rows + 8 * g).astype(F32)) / (total_rows - 1)
        q2 = jnp.zeros((8, LANES), F32)
        for c in range(CHUNKS):
            q = A[3, c, pl.ds(OWN + 8 * g, 8), :]
            q2 = q2 + q * q
        total = total + w * q2

    def add_up(step, total):
        acc[step] = total
        copy = remote(acc.at[step], got.at[step], sum_send.at[step], sum_recv.at[step], flip(sizes[step]))
        copy.wait()
        return total + got[step]

    for step in range(4):
        total = add_up(step, total)
    score[0] = jnp.sum(total) / (total_rows * state.shape[3])

    def arrived(buffer, sem):
        pltpu.make_async_copy(buffer, buffer, sem).wait()

    for i, (begin, count) in enumerate(PIECES):
        arrived(H[i].at[y_prev, 0], y_recv.at[i, 0, 0])
        on = remote(H[i].at[y_prev, 0], H[i].at[y_prev, 0], y_send.at[i, 5], y_recv.at[i, 2, 1], (member(y_next, xh, core), d))
        arrived(H[i].at[y_next, 1], y_recv.at[i, 1, 1])
        back = remote(H[i].at[y_next, 1], H[i].at[y_next, 1], y_send.at[i, 6], y_recv.at[i, 2, 2], (member(y_prev, xh, core), d))
        pending += [on, back]
    xs = []
    for i, (begin, count) in enumerate(PIECES):
        far = (y + 2) % 4
        arrived(H[i].at[y_prev, 1], y_recv.at[i, 0, 1])
        arrived(H[i].at[y_next, 0], y_recv.at[i, 1, 0])
        arrived(H[i].at[far, 0], y_recv.at[i, 2, 1])
        arrived(H[i].at[far, 1], y_recv.at[i, 2, 2])
        arrived(H[i].at[y, 1 - core], y_recv.at[i, 2, 0])
        ring[i][0].wait()
        for j in (0, 1):
            p = parents[member(y, 1 - xh, j)]
            V[i][j] = H[i][p // 4, p % 2]
            xs.append(remote(V[i].at[j], Q[i].at[j], x_send.at[i, j], x_recv.at[i, j], (x_next, x_prev)[j]))
    for i, (begin, count) in enumerate(PIECES):
        for j in (0, 1):
            arrived(Q[i].at[j], x_recv.at[i, j])
            pending.append(remote(Q[i].at[j], X[i].at[j], x_send.at[i, 2 + j], x_recv.at[i, 2 + j], (x_next, x_prev)[j]))
    swaps = []
    for i, (begin, count) in enumerate(PIECES):
        part = pl.ds(OWN + begin, count)
        for j in (0, 1):
            arrived(X[i].at[j], x_recv.at[i, 2 + j])
        p = parents[member(y, xh, 1 - core)]
        T[i][...] = jnp.where((p // 2) % 2 == xh, H[i][p // 4, p % 2], X[i][1 - core])
        swaps.append(remote(T[i], U[i], swap_send.at[i], swap_recv.at[i], other))
        p = parents[m]
        C[mine, :, part, :] = noise[mine, :, pl.ds(begin, count), :] + jnp.where(
            (p // 2) % 2 == xh, H[i][p // 4, p % 2], X[i][core])
    for i, (begin, count) in enumerate(PIECES):
        part = pl.ds(OWN + begin, count)
        swaps[i].wait()
        C[theirs, :, part, :] = noise[theirs, :, pl.ds(begin, count), :] + U[i][...]

    exchange(C, 1)
    run_steps(C)
    stores = []
    for c in range(CHUNKS):
        lanes = pl.ds(c * LANES, LANES)
        stores.append(pltpu.make_async_copy(C.at[:, c, pl.ds(OWN, rows), :], after.at[0, :, :, lanes], out_sem.at[c]))
    for store in stores:
        store.start()
    for copies in ring:
        for copy in copies[1:]:
            copy.wait_send()
    for copy in pending + xs:
        copy.wait_send()
    for store in stores:
        store.wait()


def solution(mesh):
    def on_device(state, perturbation, parents):
        rows = state.shape[2]
        buffer = pltpu.VMEM((FIELDS, CHUNKS, BUFFER_ROWS, LANES), F32)

        def each(*lead):
            return [pltpu.VMEM((*lead, 2, CHUNKS, count, LANES), F32) for _, count in PIECES]

        n = len(PIECES)
        dma = pltpu.SemaphoreType.DMA
        return pl.pallas_call(
            kernel,
            out_shape=(jax.ShapeDtypeStruct(state.shape, F32), jax.ShapeDtypeStruct((1,), F32)),
            in_specs=[
                pl.BlockSpec(memory_space=pltpu.SMEM),
                pl.BlockSpec(memory_space=pl.ANY),
                pl.BlockSpec(memory_space=pl.ANY),
            ],
            out_specs=(pl.BlockSpec(memory_space=pl.ANY), pl.BlockSpec(memory_space=pltpu.SMEM)),
            scratch_shapes=[buffer] * 4
            + [pltpu.VMEM((FIELDS, CHUNKS, rows, LANES), F32)]
            + [pltpu.VMEM((4, 8, LANES), F32)] * 2
            + each(4, 2) + each(2) + each(2) + each(2) + each() + each()
            + [dma((2, 4)), dma((2, 2)), dma((2, 2)), dma((4,)), dma((4,)), dma((4,)),
               dma((n, 8)), dma((n, 3, 3)), dma((n, 4)), dma((n, 4)), dma((n,)), dma((n,))],
            compiler_params=pltpu.CompilerParams(collective_id=0, has_side_effects=True),
        )(parents, state, perturbation)

    placed = P("member", None, "domain", None)
    return jax.shard_map(
        on_device, mesh=mesh, in_specs=(placed, placed, P()), out_specs=(placed, P("member")), check_vma=False
    )
```

```python
import jax
import jax.numpy as jnp
from jax import lax
from jax.experimental import pallas as pl
from jax.experimental.pallas import tpu as pltpu
from jax.sharding import PartitionSpec as P

F32 = jnp.float32
MESH = pl.DeviceIdType.MESH
STEPS = 3
STAGES = 3 * STEPS
time_step = 0.1
viscous = 0.05
coriolis = 1.0

FIELDS, CHUNKS, LANES = 4, 4, 128
OWN = 16
BUFFER_ROWS = 64
HALO = STAGES
PIECES = ((0, 9), (23, 9), (9, 7), (16, 7))


def stage(src, base, dst, start, groups, weight, old, lat0, lat1):
    lane = lax.broadcasted_iota(jnp.int32, (8, LANES), 1)
    row = lax.broadcasted_iota(jnp.int32, (8, LANES), 0).astype(F32)
    last, first = lane == LANES - 1, lane == 0
    keep = weight * (1.0 - 4.0 * viscous * time_step)
    spread = weight * viscous * time_step
    half = -weight * time_step * 0.5
    turn = weight * time_step * coriolis

    def body(group, carry):
        r = start + 8 * group
        here, north, south = pl.ds(r, 8), pl.ds(r + 1, 8), pl.ds(r - 1, 8)
        lat = ((row + r.astype(F32)) * lat1 + lat0) * turn
        cells = [[src[f, c, here, :] for c in range(CHUNKS)] for f in range(FIELDS)]
        to_west = [[pltpu.roll(cells[f][c], LANES - 1, 1) for c in range(CHUNKS)] for f in range(FIELDS)]
        to_east = [[pltpu.roll(cells[f][c], 1, 1) for c in range(CHUNKS)] for f in range(FIELDS)]
        for c in range(CHUNKS):
            E, W, N, S, dx, dy, out = [], [], [], [], [], [], []
            for f in range(FIELDS):
                e = jnp.where(last, to_west[f][(c + 1) % CHUNKS], to_west[f][c])
                w = jnp.where(first, to_east[f][(c - 1) % CHUNKS], to_east[f][c])
                n, s = src[f, c, north, :], src[f, c, south, :]
                E.append(e)
                W.append(w)
                N.append(n)
                S.append(s)
                dx.append(e - w)
                dy.append(n - s)
                o = keep * cells[f][c] + spread * ((e + w) + (n + s))
                if base is not None:
                    o = o + old * base[f, c, here, :]
                out.append(o)
            u, v = cells[1][c], cells[2][c]
            us, vs = half * u, half * v
            flux = (E[0] * E[1] - W[0] * W[1]) + (N[0] * N[2] - S[0] * S[2]) + (dx[1] + dy[2])
            dst[0, c, here, :] = out[0] + half * flux
            dst[1, c, here, :] = out[1] + (us * dx[1] + vs * dy[1]) + (lat * v + half * dx[0])
            dst[2, c, here, :] = out[2] + (us * dx[2] + vs * dy[2]) + (half * dy[0] - lat * u)
            dst[3, c, here, :] = out[3] + (us * dx[3] + vs * dy[3])
        return carry

    lax.fori_loop(0, groups, body, 0)


def kernel(
    parents, state, perturbation, after, score,
    A, C, S1, S2, noise, acc, got, *rest,
):
    pieces = len(PIECES)
    H, V, X, T, U = (rest[i * pieces:(i + 1) * pieces] for i in range(5))
    (load_sem, halo_send, halo_recv, sum_send, sum_recv,
     y_send, y_recv, x_send, x_recv, swap_send, swap_recv) = rest[5 * pieces:]
    m, d = lax.axis_index("member"), lax.axis_index("domain")
    y, xh, core = m // 4, (m // 2) % 2, m % 2
    xl, z = d // 8, d % 8
    rows = state.shape[2]
    domains = 16
    total_rows = rows * domains

    def member(y_, xh_, core_):
        return (y_ * 2 + xh_) * 2 + core_

    y_next, y_prev = (y + 1) % 4, (y + 3) % 4
    across = (member(y, 1 - xh, core), d)
    other = (member(y, xh, 1 - core), d)
    d_next, d_prev = (m, (d + 1) % domains), (m, (d + domains - 1) % domains)

    def flip(size):
        return (m, d + size - 2 * size * ((d // size) % 2))

    sizes = (1, 2, 4, 8)
    greeted = [d_next, d_prev, across, other] + [flip(s) for s in sizes]
    greeted += [(member(yy, xh, k), d) for yy in (y_next, y_prev) for k in (0, 1)]

    loads = []
    for c in range(CHUNKS):
        lanes = pl.ds(c * LANES, LANES)
        loads.append(pltpu.make_async_copy(state.at[0, :, :, lanes], A.at[:, c, pl.ds(OWN, rows), :], load_sem.at[0, c]))
    for c in range(CHUNKS):
        lanes = pl.ds(c * LANES, LANES)
        loads.append(pltpu.make_async_copy(perturbation.at[0, :, :, lanes], noise.at[:, c, :, :], load_sem.at[1, c]))
    for load in loads:
        load.start()

    barrier = pltpu.get_barrier_semaphore()
    for device in greeted:
        pl.semaphore_signal(barrier, inc=1, device_id=device, device_id_type=MESH)
    pl.semaphore_wait(barrier, len(greeted))

    def remote(src, dst, send, recv, device):
        copy = pltpu.make_async_remote_copy(
            src_ref=src, dst_ref=dst, send_sem=send, recv_sem=recv, device_id=device, device_id_type=MESH
        )
        copy.start()
        return copy

    def send_south(B, which):
        return remote(B.at[:, :, pl.ds(OWN, HALO), :], B.at[:, :, pl.ds(OWN + rows, HALO), :],
                      halo_send.at[which, 0], halo_recv.at[which, 0], d_prev)

    def send_north(B, which):
        return remote(B.at[:, :, pl.ds(OWN + rows - HALO, HALO), :], B.at[:, :, pl.ds(OWN - HALO, HALO), :],
                      halo_send.at[which, 1], halo_recv.at[which, 1], d_next)

    nothing = jnp.zeros((FIELDS, CHUNKS, 8, LANES), F32)

    def clear_ends(B):
        @pl.when(d == 0)
        def _():
            B[:, :, pl.ds(OWN - 8, 8), :] = nothing

        @pl.when(d == domains - 1)
        def _():
            B[:, :, pl.ds(OWN + rows, 8), :] = nothing

    first_row = (d * rows - OWN).astype(F32)
    lat0 = 2.0 * (first_row + 0.5) / total_rows - 1.0
    lat1 = 2.0 / total_rows

    def run_steps(B, result):
        clear_ends(B)
        for k in range(1, STAGES + 1):
            groups = -(-(rows + 2 * (STAGES - k)) // 8)
            src, base, dst, weight, old = (
                (B, None, S1, 1.0, 0.0), (S1, B, S2, 0.25, 0.75), (S2, B, B, 2.0 / 3.0, 1.0 / 3.0)
            )[(k - 1) % 3]
            if k == STAGES:
                dst = result
            stage(src, base, dst, OWN - STAGES + k, groups, weight, old, lat0, lat1)
            if k < STAGES:
                clear_ends(dst)

    for load in loads:
        load.wait()
    halos = [send_south(A, 0), send_north(A, 0)]
    for halo in halos:
        halo.wait()
    run_steps(A, A)

    weight_row = lax.broadcasted_iota(jnp.int32, (8, LANES), 0).astype(F32)
    partial = [jnp.zeros((8, LANES), F32)]
    for g in range(rows // 8):
        w = 1.0 + 2.0 * (weight_row + (d * rows + 8 * g).astype(F32)) / (total_rows - 1)
        q2 = jnp.zeros((8, LANES), F32)
        for c in range(CHUNKS):
            q = A[3, c, pl.ds(OWN + 8 * g, 8), :]
            q2 = q2 + q * q
        partial[0] = partial[0] + w * q2
    sums = []

    def add_up():
        if sums:
            step = len(sums) - 1
            sums[-1].wait()
            partial[0] = partial[0] + got[step]
        step = len(sums)
        if step < len(sizes):
            acc[step] = partial[0]
            sums.append(remote(acc.at[step], got.at[step], sum_send.at[step], sum_recv.at[step], flip(sizes[step])))

    mine, theirs = pl.ds(2 * core, 2), pl.ds(2 * (1 - core), 2)
    far = (y + 2) % 4
    sent, local, swaps = [], [None] * pieces, [None] * pieces

    def arrived(buffer, sem):
        pltpu.make_async_copy(buffer, buffer, sem).wait()

    def ring(i):
        part = pl.ds(OWN + PIECES[i][0], PIECES[i][1])
        place = H[i].at[y, core]
        for way, yy in enumerate((y_next, y_prev)):
            for k in (0, 1):
                sent.append(remote(A.at[pl.ds(2 * k, 2), :, part, :], place, y_send.at[i, 2 * way + k],
                                   y_recv.at[i, way, core], (member(yy, xh, k), d)))
        sent.append(remote(A.at[theirs, :, part, :], place, y_send.at[i, 4], y_recv.at[i, 2, 0], other))
        local[i] = pltpu.make_async_copy(A.at[mine, :, part, :], place, y_send.at[i, 7])
        local[i].start()

    def forward(i):
        for way, (block, yy) in enumerate(((H[i].at[y_prev, 0], y_next), (H[i].at[y_next, 1], y_prev))):
            arrived(block, y_recv.at[i, way, way])
            sent.append(remote(block, block, y_send.at[i, 5 + way], y_recv.at[i, 2, 1 + way], (member(yy, xh, core), d)))

    def choose(i):
        arrived(H[i].at[y_prev, 1], y_recv.at[i, 0, 1])
        arrived(H[i].at[y_next, 0], y_recv.at[i, 1, 0])
        arrived(H[i].at[y, 1 - core], y_recv.at[i, 2, 0])
        local[i].wait()
        arrived(H[i].at[far, 0], y_recv.at[i, 2, 1])
        arrived(H[i].at[far, 1], y_recv.at[i, 2, 2])
        for j in (0, 1):
            p = parents[member(y, 1 - xh, j)]
            V[i][j] = H[i][p // 4, p % 2]
        sent.append(remote(V[i], X[i], x_send.at[i], x_recv.at[i], across))

    def swap(i):
        begin, count = PIECES[i]
        arrived(X[i], x_recv.at[i])
        p = parents[member(y, xh, 1 - core)]
        T[i][...] = jnp.where((p // 2) % 2 == xh, H[i][p // 4, p % 2], X[i][1 - core])
        swaps[i] = remote(T[i], U[i], swap_send.at[i], swap_recv.at[i], other)
        p = parents[m]
        C[mine, :, pl.ds(OWN + begin, count), :] = noise[mine, :, pl.ds(begin, count), :] + jnp.where(
            (p // 2) % 2 == xh, H[i][p // 4, p % 2], X[i][core])

    def finish(i):
        begin, count = PIECES[i]
        swaps[i].wait()
        C[theirs, :, pl.ds(OWN + begin, count), :] = noise[theirs, :, pl.ds(begin, count), :] + U[i][...]

    ring(0)
    ring(1)
    ring(2)
    add_up()
    forward(0)
    ring(3)
    forward(1)
    add_up()
    choose(0)
    forward(2)
    choose(1)
    swap(0)
    add_up()
    forward(3)
    finish(0)
    halos = [send_south(C, 1)]
    choose(2)
    swap(1)
    finish(1)
    halos.append(send_north(C, 1))
    add_up()
    choose(3)
    swap(2)
    finish(2)
    add_up()
    score[0] = jnp.sum(partial[0]) / (total_rows * state.shape[3])
    swap(3)
    finish(3)
    for halo in halos:
        halo.wait()

    class Result:
        def __setitem__(self, at, value):
            f, c, here, _ = at
            after[0, f, pl.ds(pl.multiple_of(here.start - OWN, 8), here.size), pl.ds(c * LANES, LANES)] = value

    run_steps(C, Result())
    for copy in sent:
        copy.wait_send()


def solution(mesh):
    def on_device(state, perturbation, parents):
        rows = state.shape[2]
        buffer = pltpu.VMEM((FIELDS, CHUNKS, BUFFER_ROWS, LANES), F32)

        def each(*lead):
            return [pltpu.VMEM((*lead, 2, CHUNKS, count, LANES), F32) for _, count in PIECES]

        n = len(PIECES)
        dma = pltpu.SemaphoreType.DMA
        return pl.pallas_call(
            kernel,
            out_shape=(pltpu.VMEM(state.shape, F32), jax.ShapeDtypeStruct((1,), F32)),
            in_specs=[
                pl.BlockSpec(memory_space=pltpu.SMEM),
                pl.BlockSpec(memory_space=pl.ANY),
                pl.BlockSpec(memory_space=pl.ANY),
            ],
            out_specs=(pl.BlockSpec(memory_space=pltpu.VMEM), pl.BlockSpec(memory_space=pltpu.SMEM)),
            scratch_shapes=[buffer] * 4
            + [pltpu.VMEM((FIELDS, CHUNKS, rows, LANES), F32)]
            + [pltpu.VMEM((4, 8, LANES), F32)] * 2
            + each(4, 2) + each(2) + each(2) + each() + each()
            + [dma((2, 4)), dma((2, 2)), dma((2, 2)), dma((4,)), dma((4,)),
               dma((n, 8)), dma((n, 3, 3)), dma((n,)), dma((n,)), dma((n,)), dma((n,))],
            compiler_params=pltpu.CompilerParams(collective_id=0, has_side_effects=True),
        )(parents, state, perturbation)

    placed = P("member", None, "domain", None)
    return jax.shard_map(
        on_device, mesh=mesh, in_specs=(placed, placed, P()), out_specs=(placed, P("member")), check_vma=False
    )
```

```python
import jax
import jax.numpy as jnp
from jax import lax
from jax.experimental import pallas as pl
from jax.experimental.pallas import tpu as pltpu
from jax.sharding import PartitionSpec as P

F32 = jnp.float32
MESH = pl.DeviceIdType.MESH
STEPS = 3
STAGES = 3 * STEPS
time_step = 0.1
viscous = 0.05
coriolis = 1.0

FIELDS, CHUNKS, LANES = 4, 4, 128
OWN = 16
BUFFER_ROWS = 64
HALO = STAGES
MIDDLE, TOP, BOTTOM = 0, 1, 2
PIECES = ((9, 14), (0, 9), (23, 9))


def stage(src, base, dst, start, rows, weight, old, lat0, lat1, shift=0):
    lane = lax.broadcasted_iota(jnp.int32, (8, LANES), 1)
    row = lax.broadcasted_iota(jnp.int32, (8, LANES), 0).astype(F32)
    last, first = lane == LANES - 1, lane == 0
    keep = weight * (1.0 - 4.0 * viscous * time_step)
    spread = weight * viscous * time_step
    half = -weight * time_step * 0.5
    turn = weight * time_step * coriolis

    def body(group, carry):
        r = jnp.minimum(start + 8 * group, start + rows - 8)
        here, north, south = pl.ds(r, 8), pl.ds(r + 1, 8), pl.ds(r - 1, 8)
        there = pl.ds(r - shift, 8)
        lat = ((row + r.astype(F32)) * lat1 + lat0) * turn
        cells = [[src[f, c, here, :] for c in range(CHUNKS)] for f in range(FIELDS)]
        to_west = [[pltpu.roll(cells[f][c], LANES - 1, 1) for c in range(CHUNKS)] for f in range(FIELDS)]
        to_east = [[pltpu.roll(cells[f][c], 1, 1) for c in range(CHUNKS)] for f in range(FIELDS)]
        for c in range(CHUNKS):
            E, W, N, S, dx, dy, out = [], [], [], [], [], [], []
            for f in range(FIELDS):
                e = jnp.where(last, to_west[f][(c + 1) % CHUNKS], to_west[f][c])
                w = jnp.where(first, to_east[f][(c - 1) % CHUNKS], to_east[f][c])
                n, s = src[f, c, north, :], src[f, c, south, :]
                E.append(e)
                W.append(w)
                N.append(n)
                S.append(s)
                dx.append(e - w)
                dy.append(n - s)
                o = keep * cells[f][c] + spread * ((e + w) + (n + s))
                if base is not None:
                    o = o + old * base[f, c, here, :]
                out.append(o)
            u, v = cells[1][c], cells[2][c]
            us, vs = half * u, half * v
            flux = (E[0] * E[1] - W[0] * W[1]) + (N[0] * N[2] - S[0] * S[2]) + (dx[1] + dy[2])
            dst[0, c, there, :] = out[0] + half * flux
            dst[1, c, there, :] = out[1] + (us * dx[1] + vs * dy[1]) + (lat * v + half * dx[0])
            dst[2, c, there, :] = out[2] + (us * dx[2] + vs * dy[2]) + (half * dy[0] - lat * u)
            dst[3, c, there, :] = out[3] + (us * dx[3] + vs * dy[3])
        return carry

    lax.fori_loop(0, -(-rows // 8), body, 0)


def kernel(
    parents, state, perturbation, after, score,
    A, C, Y, top, bottom, noise, acc, got, *rest,
):
    pieces = len(PIECES)
    H, V, X, T, U = (rest[i * pieces:(i + 1) * pieces] for i in range(5))
    (load_sem, halo_send, halo_recv, sum_send, sum_recv,
     y_send, y_recv, x_send, x_recv, swap_send, swap_recv) = rest[5 * pieces:]
    m, d = lax.axis_index("member"), lax.axis_index("domain")
    y, xh, core = m // 4, (m // 2) % 2, m % 2
    xl, z = d // 8, d % 8
    rows = state.shape[2]
    domains = 16
    total_rows = rows * domains

    def member(y_, xh_, core_):
        return (y_ * 2 + xh_) * 2 + core_

    y_next, y_prev = (y + 1) % 4, (y + 3) % 4
    across = (member(y, 1 - xh, core), d)
    other = (member(y, xh, 1 - core), d)
    d_next, d_prev = (m, (d + 1) % domains), (m, (d + domains - 1) % domains)

    def flip(size):
        return (m, d + size - 2 * size * ((d // size) % 2))

    sizes = (4, 8, 2, 1)
    greeted = [d_next, d_prev, across, other] + [flip(s) for s in sizes]
    greeted += [(member(yy, xh, k), d) for yy in (y_next, y_prev) for k in (0, 1)]

    loads = []
    for c in range(CHUNKS):
        lanes = pl.ds(c * LANES, LANES)
        loads.append(pltpu.make_async_copy(state.at[0, :, :, lanes], A.at[:, c, pl.ds(OWN, rows), :], load_sem.at[0, c]))
    for c in range(CHUNKS):
        lanes = pl.ds(c * LANES, LANES)
        loads.append(pltpu.make_async_copy(perturbation.at[0, :, :, lanes], noise.at[:, c, :, :], load_sem.at[1, c]))
    for load in loads:
        load.start()

    barrier = pltpu.get_barrier_semaphore()
    for device in greeted:
        pl.semaphore_signal(barrier, inc=1, device_id=device, device_id_type=MESH)
    pl.semaphore_wait(barrier, len(greeted))

    def remote(src, dst, send, recv, device):
        copy = pltpu.make_async_remote_copy(
            src_ref=src, dst_ref=dst, send_sem=send, recv_sem=recv, device_id=device, device_id_type=MESH
        )
        copy.start()
        return copy

    def send_south(B, which):
        return remote(B.at[:, :, pl.ds(OWN, HALO), :], B.at[:, :, pl.ds(OWN + rows, HALO), :],
                      halo_send.at[which, 0], halo_recv.at[which, 0], d_prev)

    def send_north(B, which):
        return remote(B.at[:, :, pl.ds(OWN + rows - HALO, HALO), :], B.at[:, :, pl.ds(OWN - HALO, HALO), :],
                      halo_send.at[which, 1], halo_recv.at[which, 1], d_next)

    first_row = (d * rows - OWN).astype(F32)
    lat0 = 2.0 * (first_row + 0.5) / total_rows - 1.0
    lat1 = 2.0 / total_rows
    nothing = jnp.zeros((FIELDS, CHUNKS, 8, LANES), F32)

    def clear_south(B):
        @pl.when(d == 0)
        def _():
            B[:, :, pl.ds(OWN - 8, 8), :] = nothing

    def clear_north(B):
        @pl.when(d == domains - 1)
        def _():
            B[:, :, pl.ds(OWN + rows, 8), :] = nothing

    def run(B, first, count, k, dst=None, shift=0):
        levels = [B] + [Y.at[i] for i in range(STAGES)]
        weight, old = ((1.0, 0.0), (0.25, 0.75), (2.0 / 3.0, 1.0 / 3.0))[(k - 1) % 3]
        base = levels[k - 1 - (k - 1) % 3] if old else None
        stage(levels[k - 1], base, dst if dst is not None else levels[k], OWN + first, count, weight, old, lat0, lat1, shift)

    def inside(B, until, stages):
        for k in stages:
            run(B, k, until - 2 * k, k)

    def south(B, result, shift):
        clear_south(B)
        for k in range(1, STAGES):
            run(B, k - STAGES, 16, k)
            clear_south(Y.at[k - 1])
        run(B, 0, 16, STAGES, result, shift)

    def north(B, wide, result, shift):
        clear_north(B)
        for k in range(1, STAGES):
            run(B, rows + STAGES - k - wide, wide, k)
            clear_north(Y.at[k - 1])
        run(B, rows - 16, 16, STAGES, result, shift)

    for load in loads[:CHUNKS]:
        load.wait()
    halos = [send_south(A, 0), send_north(A, 0)]
    inside(A, rows, range(1, STAGES + 1))

    sums, partial = [], []

    def weigh():
        row = lax.broadcasted_iota(jnp.int32, (8, LANES), 0).astype(F32)
        total = jnp.zeros((8, LANES), F32)
        for g in range(rows // 8):
            weight = 1.0 + 2.0 * (row + (d * rows + 8 * g).astype(F32)) / (total_rows - 1)
            squares = jnp.zeros((8, LANES), F32)
            for c in range(CHUNKS):
                q = (top, bottom)[g // 2][3, c, pl.ds(8 * (g % 2), 8), :]
                squares = squares + q * q
            total = total + weight * squares
        partial.append(total)

    def add_up():
        if sums:
            step = len(sums) - 1
            sums[-1].wait()
            partial[0] = partial[0] + got[step]
        step = len(sums)
        if step < len(sizes):
            acc[step] = partial[0]
            sums.append(remote(acc.at[step], got.at[step], sum_send.at[step], sum_recv.at[step], flip(sizes[step])))

    mine, theirs = pl.ds(2 * core, 2), pl.ds(2 * (1 - core), 2)
    far = (y + 2) % 4
    sent, local, swaps = [], [None] * pieces, [None] * pieces

    def arrived(buffer, sem):
        pltpu.make_async_copy(buffer, buffer, sem).wait()

    def ring(i):
        A, begin = ((Y.at[STAGES - 1], OWN + PIECES[i][0]), (top, 0), (bottom, 16 - PIECES[i][1]))[i]
        part = pl.ds(begin, PIECES[i][1])
        place = H[i].at[y, core]
        for way, yy in enumerate((y_next, y_prev)):
            for k in (0, 1):
                sent.append(remote(A.at[pl.ds(2 * k, 2), :, part, :], place, y_send.at[i, 2 * way + k],
                                   y_recv.at[i, way, core], (member(yy, xh, k), d)))
        sent.append(remote(A.at[theirs, :, part, :], place, y_send.at[i, 4], y_recv.at[i, 2, 0], other))
        local[i] = pltpu.make_async_copy(A.at[mine, :, part, :], place, y_send.at[i, 7])
        local[i].start()

    def forward(i):
        for way, (block, yy) in enumerate(((H[i].at[y_prev, 0], y_next), (H[i].at[y_next, 1], y_prev))):
            arrived(block, y_recv.at[i, way, way])
            sent.append(remote(block, block, y_send.at[i, 5 + way], y_recv.at[i, 2, 1 + way], (member(yy, xh, core), d)))

    def choose(i):
        arrived(H[i].at[y_prev, 1], y_recv.at[i, 0, 1])
        arrived(H[i].at[y_next, 0], y_recv.at[i, 1, 0])
        arrived(H[i].at[y, 1 - core], y_recv.at[i, 2, 0])
        local[i].wait()
        arrived(H[i].at[far, 0], y_recv.at[i, 2, 1])
        arrived(H[i].at[far, 1], y_recv.at[i, 2, 2])
        for j in (0, 1):
            p = parents[member(y, 1 - xh, j)]
            V[i][j] = H[i][p // 4, p % 2]
        sent.append(remote(V[i], X[i], x_send.at[i], x_recv.at[i], across))

    def swap(i):
        begin, count = PIECES[i]
        arrived(X[i], x_recv.at[i])
        p = parents[member(y, xh, 1 - core)]
        T[i][...] = jnp.where((p // 2) % 2 == xh, H[i][p // 4, p % 2], X[i][1 - core])
        swaps[i] = remote(T[i], U[i], swap_send.at[i], swap_recv.at[i], other)
        p = parents[m]
        C[mine, :, pl.ds(OWN + begin, count), :] = noise[mine, :, pl.ds(begin, count), :] + jnp.where(
            (p // 2) % 2 == xh, H[i][p // 4, p % 2], X[i][core])

    def finish(i):
        begin, count = PIECES[i]
        swaps[i].wait()
        C[theirs, :, pl.ds(OWN + begin, count), :] = noise[theirs, :, pl.ds(begin, count), :] + U[i][...]

    ring(MIDDLE)
    halos[1].wait()
    south(A, top, OWN)
    ring(TOP)
    forward(MIDDLE)
    halos[0].wait()
    north(A, 16, bottom, OWN + 16)
    ring(BOTTOM)
    forward(TOP)
    weigh()
    add_up()
    choose(MIDDLE)
    choose(TOP)
    forward(BOTTOM)
    for load in loads[CHUNKS:]:
        load.wait()
    swap(MIDDLE)
    swap(TOP)
    choose(BOTTOM)
    finish(MIDDLE)
    finish(TOP)
    halos = [send_south(C, 1)]
    add_up()
    inside(C, PIECES[BOTTOM][0], range(1, STAGES))
    swap(BOTTOM)
    finish(BOTTOM)
    halos.append(send_north(C, 1))
    add_up()

    class Result:
        def __setitem__(self, at, value):
            f, c, here, _ = at
            after[0, f, pl.ds(pl.multiple_of(here.start, 8), here.size), pl.ds(c * LANES, LANES)] = value

    halos[0].wait()
    north(C, 24, Result(), OWN)
    add_up()
    halos[1].wait()
    south(C, Result(), OWN)
    add_up()
    score[0] = jnp.sum(partial[0]) / (total_rows * state.shape[3])
    for copy in sent:
        copy.wait_send()


def solution(mesh):
    def on_device(state, perturbation, parents):
        rows = state.shape[2]
        buffer = pltpu.VMEM((FIELDS, CHUNKS, BUFFER_ROWS, LANES), F32)

        def each(*lead):
            return [pltpu.VMEM((*lead, 2, CHUNKS, count, LANES), F32) for _, count in PIECES]

        n = len(PIECES)
        dma = pltpu.SemaphoreType.DMA
        return pl.pallas_call(
            kernel,
            out_shape=(pltpu.VMEM(state.shape, F32), jax.ShapeDtypeStruct((1,), F32)),
            in_specs=[
                pl.BlockSpec(memory_space=pltpu.SMEM),
                pl.BlockSpec(memory_space=pl.ANY),
                pl.BlockSpec(memory_space=pl.ANY),
            ],
            out_specs=(pl.BlockSpec(memory_space=pltpu.VMEM), pl.BlockSpec(memory_space=pltpu.SMEM)),
            scratch_shapes=[buffer] * 2
            + [pltpu.VMEM((STAGES, FIELDS, CHUNKS, BUFFER_ROWS, LANES), F32)]
            + [pltpu.VMEM((FIELDS, CHUNKS, 16, LANES), F32)] * 2
            + [pltpu.VMEM((FIELDS, CHUNKS, rows, LANES), F32)]
            + [pltpu.VMEM((4, 8, LANES), F32)] * 2
            + each(4, 2) + each(2) + each(2) + each() + each()
            + [dma((2, 4)), dma((2, 2)), dma((2, 2)), dma((4,)), dma((4,)),
               dma((n, 8)), dma((n, 3, 3)), dma((n,)), dma((n,)), dma((n,)), dma((n,))],
            compiler_params=pltpu.CompilerParams(collective_id=0, has_side_effects=True),
        )(parents, state, perturbation)

    placed = P("member", None, "domain", None)
    return jax.shard_map(
        on_device, mesh=mesh, in_specs=(placed, placed, P()), out_specs=(placed, P("member")), check_vma=False
    )
```

```python
import jax
import jax.numpy as jnp
from jax import lax
from jax.experimental import pallas as pl
from jax.experimental.pallas import tpu as pltpu
from jax.sharding import PartitionSpec as P

F32 = jnp.float32
MESH = pl.DeviceIdType.MESH
STEPS = 3
STAGES = 3 * STEPS
time_step = 0.1
viscous = 0.05
coriolis = 1.0

FIELDS, CHUNKS, LANES = 4, 4, 128
OWN = 16
BUFFER_ROWS = 64
HALO = STAGES
MIDDLE, TOP, BOTTOM = 0, 1, 2
PIECES = ((9, 14), (0, 9), (23, 9))


def stage(src, base, dst, start, rows, weight, old, lat0, lat1, shift=0):
    lane = lax.broadcasted_iota(jnp.int32, (8, LANES), 1)
    row = lax.broadcasted_iota(jnp.int32, (8, LANES), 0).astype(F32)
    last, first = lane == LANES - 1, lane == 0
    keep = weight * (1.0 - 4.0 * viscous * time_step)
    spread = weight * viscous * time_step
    half = -weight * time_step * 0.5
    turn = weight * time_step * coriolis

    def body(group, carry):
        r = jnp.minimum(start + 8 * group, start + rows - 8)
        here, north, south = pl.ds(r, 8), pl.ds(r + 1, 8), pl.ds(r - 1, 8)
        there = pl.ds(r - shift, 8)
        lat = ((row + r.astype(F32)) * lat1 + lat0) * turn
        cells = [[src[f, c, here, :] for c in range(CHUNKS)] for f in range(FIELDS)]
        to_west = [[pltpu.roll(cells[f][c], LANES - 1, 1) for c in range(CHUNKS)] for f in range(FIELDS)]
        to_east = [[pltpu.roll(cells[f][c], 1, 1) for c in range(CHUNKS)] for f in range(FIELDS)]
        for c in range(CHUNKS):
            E, W, N, S, dx, dy, out = [], [], [], [], [], [], []
            for f in range(FIELDS):
                e = jnp.where(last, to_west[f][(c + 1) % CHUNKS], to_west[f][c])
                w = jnp.where(first, to_east[f][(c - 1) % CHUNKS], to_east[f][c])
                n, s = src[f, c, north, :], src[f, c, south, :]
                E.append(e)
                W.append(w)
                N.append(n)
                S.append(s)
                dx.append(e - w)
                dy.append(n - s)
                o = keep * cells[f][c] + spread * ((e + w) + (n + s))
                if base is not None:
                    o = o + old * base[f, c, here, :]
                out.append(o)
            u, v = cells[1][c], cells[2][c]
            us, vs = half * u, half * v
            flux = (E[0] * E[1] - W[0] * W[1]) + (N[0] * N[2] - S[0] * S[2]) + (dx[1] + dy[2])
            dst[0, c, there, :] = out[0] + half * flux
            dst[1, c, there, :] = out[1] + (us * dx[1] + vs * dy[1]) + (lat * v + half * dx[0])
            dst[2, c, there, :] = out[2] + (us * dx[2] + vs * dy[2]) + (half * dy[0] - lat * u)
            dst[3, c, there, :] = out[3] + (us * dx[3] + vs * dy[3])
        return carry

    lax.fori_loop(0, -(-rows // 8), body, 0)


def kernel(
    parents, state, perturbation, after, score,
    A, C, Y, top, bottom, noise, acc, got, *rest,
):
    pieces = len(PIECES)
    H, V, X = (rest[i * pieces:(i + 1) * pieces] for i in range(3))
    (load_sem, halo_send, halo_recv, sum_send, sum_recv,
     y_send, y_recv, x_send, x_recv) = rest[3 * pieces:]
    m, d = lax.axis_index("member"), lax.axis_index("domain")
    y, xh, core = m // 4, (m // 2) % 2, m % 2
    xl, z = d // 8, d % 8
    rows = state.shape[2]
    domains = 16
    total_rows = rows * domains

    def member(y_, xh_, core_):
        return (y_ * 2 + xh_) * 2 + core_

    y_next, y_prev = (y + 1) % 4, (y + 3) % 4
    across = [(member(y, 1 - xh, k), d) for k in (0, 1)]
    other = (member(y, xh, 1 - core), d)
    d_next, d_prev = (m, (d + 1) % domains), (m, (d + domains - 1) % domains)

    x_side, z_next, z_prev = (m, (1 - xl) * 8 + z), (m, xl * 8 + (z + 1) % 8), (m, xl * 8 + (z + 7) % 8)

    greeted = [d_next, d_prev, z_next, z_prev, x_side, other] + across
    greeted += [(member(yy, xh, k), d) for yy in (y_next, y_prev) for k in (0, 1)]

    loads = []
    for c in range(CHUNKS):
        lanes = pl.ds(c * LANES, LANES)
        loads.append(pltpu.make_async_copy(state.at[0, :, :, lanes], A.at[:, c, pl.ds(OWN, rows), :], load_sem.at[0, c]))
    for c in range(CHUNKS):
        lanes = pl.ds(c * LANES, LANES)
        loads.append(pltpu.make_async_copy(perturbation.at[0, :, :, lanes], noise.at[:, c, :, :], load_sem.at[1, c]))
    for load in loads:
        load.start()

    barrier = pltpu.get_barrier_semaphore()
    for device in greeted:
        pl.semaphore_signal(barrier, inc=1, device_id=device, device_id_type=MESH)
    pl.semaphore_wait(barrier, len(greeted))

    def remote(src, dst, send, recv, device):
        copy = pltpu.make_async_remote_copy(
            src_ref=src, dst_ref=dst, send_sem=send, recv_sem=recv, device_id=device, device_id_type=MESH
        )
        copy.start()
        return copy

    def send_south(B, which):
        return remote(B.at[:, :, pl.ds(OWN, HALO), :], B.at[:, :, pl.ds(OWN + rows, HALO), :],
                      halo_send.at[which, 0], halo_recv.at[which, 0], d_prev)

    def send_north(B, which):
        return remote(B.at[:, :, pl.ds(OWN + rows - HALO, HALO), :], B.at[:, :, pl.ds(OWN - HALO, HALO), :],
                      halo_send.at[which, 1], halo_recv.at[which, 1], d_next)

    first_row = (d * rows - OWN).astype(F32)
    lat0 = 2.0 * (first_row + 0.5) / total_rows - 1.0
    lat1 = 2.0 / total_rows
    nothing = jnp.zeros((FIELDS, CHUNKS, 8, LANES), F32)

    def clear_south(B):
        @pl.when(d == 0)
        def _():
            B[:, :, pl.ds(OWN - 8, 8), :] = nothing

    def clear_north(B):
        @pl.when(d == domains - 1)
        def _():
            B[:, :, pl.ds(OWN + rows, 8), :] = nothing

    def run(B, first, count, k, dst=None, shift=0):
        levels = [B] + [Y.at[i] for i in range(STAGES)]
        weight, old = ((1.0, 0.0), (0.25, 0.75), (2.0 / 3.0, 1.0 / 3.0))[(k - 1) % 3]
        base = levels[k - 1 - (k - 1) % 3] if old else None
        stage(levels[k - 1], base, dst if dst is not None else levels[k], OWN + first, count, weight, old, lat0, lat1, shift)

    def inside(B, until, stages):
        for k in stages:
            run(B, k, until - 2 * k, k)

    def south(B, result, shift):
        clear_south(B)
        for k in range(1, STAGES):
            run(B, k - STAGES, 16, k)
            clear_south(Y.at[k - 1])
        run(B, 0, 16, STAGES, result, shift)

    def north(B, wide, result, shift, meanwhile={}):
        clear_north(B)
        for k in range(1, STAGES):
            run(B, rows + STAGES - k - wide, wide, k)
            clear_north(Y.at[k - 1])
            if k in meanwhile:
                meanwhile[k]()
        run(B, rows - 16, 16, STAGES, result, shift)

    for load in loads[:CHUNKS]:
        load.wait()
    halos = [send_south(A, 0), send_north(A, 0)]
    inside(A, rows, range(1, STAGES + 1))

    sums = []

    def weigh():
        row = lax.broadcasted_iota(jnp.int32, (8, LANES), 0).astype(F32)
        total = jnp.zeros((8, LANES), F32)
        for g in range(rows // 8):
            weight = 1.0 + 2.0 * (row + (d * rows + 8 * g).astype(F32)) / (total_rows - 1)
            squares = jnp.zeros((8, LANES), F32)
            for c in range(CHUNKS):
                q = (top, bottom)[g // 2][3, c, pl.ds(8 * (g % 2), 8), :]
                squares = squares + q * q
            total = total + weight * squares
        acc[0] = total

    def add_up():
        step = len(sums)
        for copy in sums[-1] if sums else ():
            copy.wait()
        if step == 0:
            sums.append([remote(acc.at[0], acc.at[1], sum_send.at[0, 0], sum_recv.at[0, 0], x_side)])
            return
        if step == 1:
            got[z] = acc[0] + acc[1]
        if step <= 4:
            ways = ((z_next, (z + 9 - step) % 8), (z_prev, (z + step - 1) % 8))
            sums.append([remote(got.at[slot], got.at[slot], sum_send.at[step, way], sum_recv.at[step, way], device)
                         for way, (device, slot) in enumerate(ways[:1] if step == 4 else ways)])

    mine, theirs = pl.ds(2 * core, 2), pl.ds(2 * (1 - core), 2)
    far = (y + 2) % 4
    sent, local = [], [None] * pieces

    def arrived(buffer, sem):
        pltpu.make_async_copy(buffer, buffer, sem).wait()

    def ring(i):
        A, begin = ((Y.at[STAGES - 1], OWN + PIECES[i][0]), (top, 0), (bottom, 16 - PIECES[i][1]))[i]
        part = pl.ds(begin, PIECES[i][1])
        place = H[i].at[y, core]
        for way, yy in enumerate((y_next, y_prev)):
            for k in (0, 1):
                sent.append(remote(A.at[pl.ds(2 * k, 2), :, part, :], place, y_send.at[i, 2 * way + k],
                                   y_recv.at[i, way, core], (member(yy, xh, k), d)))
        sent.append(remote(A.at[theirs, :, part, :], place, y_send.at[i, 4], y_recv.at[i, 2, 0], other))
        local[i] = pltpu.make_async_copy(A.at[mine, :, part, :], place, y_send.at[i, 7])
        local[i].start()

    def forward(i):
        for way, (block, yy) in enumerate(((H[i].at[y_prev, 0], y_next), (H[i].at[y_next, 1], y_prev))):
            arrived(block, y_recv.at[i, way, way])
            sent.append(remote(block, block, y_send.at[i, 5 + way], y_recv.at[i, 2, 1 + way], (member(yy, xh, core), d)))

    def choose(i):
        arrived(H[i].at[y_prev, 1], y_recv.at[i, 0, 1])
        arrived(H[i].at[y_next, 0], y_recv.at[i, 1, 0])
        arrived(H[i].at[y, 1 - core], y_recv.at[i, 2, 0])
        local[i].wait()
        arrived(H[i].at[far, 0], y_recv.at[i, 2, 1])
        arrived(H[i].at[far, 1], y_recv.at[i, 2, 2])
        for j, (home, device) in enumerate(((1 - xh, across[0]), (1 - xh, across[1]), (xh, other))):
            p = parents[member(y, home, (0, 1, 1 - core)[j])]
            V[i][j] = H[i][p // 4, p % 2]
            slot = 2 if j == 2 else core
            sent.append(remote(V[i].at[j], X[i].at[slot], x_send.at[i, j], x_recv.at[i, slot], device))

    def take(i):
        begin, count = PIECES[i]
        for slot in range(3):
            arrived(X[i].at[slot], x_recv.at[i, slot])
        p = parents[m]
        near = (p // 2) % 2 == xh
        into, add = pl.ds(OWN + begin, count), pl.ds(begin, count)
        C[mine, :, into, :] = noise[mine, :, add, :] + jnp.where(near, H[i][p // 4, p % 2], X[i][core])
        C[theirs, :, into, :] = noise[theirs, :, add, :] + jnp.where(near, X[i][2], X[i][1 - core])

    ring(MIDDLE)
    halos[1].wait()
    south(A, top, OWN)
    ring(TOP)
    halos[0].wait()
    north(A, 16, bottom, OWN + 16, {5: lambda: forward(MIDDLE)})
    ring(BOTTOM)
    forward(TOP)
    weigh()
    add_up()
    choose(MIDDLE)
    forward(BOTTOM)
    choose(TOP)
    add_up()
    choose(BOTTOM)
    for load in loads[CHUNKS:]:
        load.wait()
    take(MIDDLE)
    take(TOP)
    halos = [send_south(C, 1)]
    add_up()
    inside(C, PIECES[BOTTOM][0], range(1, STAGES))
    take(BOTTOM)
    halos.append(send_north(C, 1))
    add_up()

    class Result:
        def __setitem__(self, at, value):
            f, c, here, _ = at
            after[0, f, pl.ds(pl.multiple_of(here.start, 8), here.size), pl.ds(c * LANES, LANES)] = value

    halos[0].wait()
    north(C, 24, Result(), OWN)
    add_up()
    halos[1].wait()
    south(C, Result(), OWN)
    add_up()
    total = got[0]
    for other_z in range(1, 8):
        total = total + got[other_z]
    score[0] = jnp.sum(total) / (total_rows * state.shape[3])
    for copy in sent:
        copy.wait_send()


def solution(mesh):
    def on_device(state, perturbation, parents):
        rows = state.shape[2]
        buffer = pltpu.VMEM((FIELDS, CHUNKS, BUFFER_ROWS, LANES), F32)

        def each(*lead):
            return [pltpu.VMEM((*lead, 2, CHUNKS, count, LANES), F32) for _, count in PIECES]

        n = len(PIECES)
        dma = pltpu.SemaphoreType.DMA
        return pl.pallas_call(
            kernel,
            out_shape=(pltpu.VMEM(state.shape, F32), jax.ShapeDtypeStruct((1,), F32)),
            in_specs=[
                pl.BlockSpec(memory_space=pltpu.SMEM),
                pl.BlockSpec(memory_space=pl.ANY),
                pl.BlockSpec(memory_space=pl.ANY),
            ],
            out_specs=(pl.BlockSpec(memory_space=pltpu.VMEM), pl.BlockSpec(memory_space=pltpu.SMEM)),
            scratch_shapes=[buffer] * 2
            + [pltpu.VMEM((STAGES, FIELDS, CHUNKS, BUFFER_ROWS, LANES), F32)]
            + [pltpu.VMEM((FIELDS, CHUNKS, 16, LANES), F32)] * 2
            + [pltpu.VMEM((FIELDS, CHUNKS, rows, LANES), F32)]
            + [pltpu.VMEM((2, 8, LANES), F32), pltpu.VMEM((8, 8, LANES), F32)]
            + each(4, 2) + each(3) + each(3)
            + [dma((2, 4)), dma((2, 2)), dma((2, 2)), dma((5, 2)), dma((5, 2)),
               dma((n, 8)), dma((n, 3, 3)), dma((n, 3)), dma((n, 3))],
            compiler_params=pltpu.CompilerParams(collective_id=0, has_side_effects=True),
        )(parents, state, perturbation)

    placed = P("member", None, "domain", None)
    return jax.shard_map(
        on_device, mesh=mesh, in_specs=(placed, placed, P()), out_specs=(placed, P("member")), check_vma=False
    )
```

```python
import jax
import jax.numpy as jnp
from jax import lax
from jax.experimental import pallas as pl
from jax.experimental.pallas import tpu as pltpu
from jax.sharding import PartitionSpec as P

F32 = jnp.float32
MESH = pl.DeviceIdType.MESH
STEPS = 3
STAGES = 3 * STEPS
time_step = 0.1
viscous = 0.05
coriolis = 1.0

FIELDS, CHUNKS, LANES = 4, 4, 128
OWN = 16
BUFFER_ROWS = 64
HALO = STAGES
MIDDLE, TOP, BOTTOM = 0, 1, 2
PIECES = ((9, 14), (0, 9), (23, 9))


def stage(src, base, dst, start, rows, weight, old, lat0, lat1, shift=0, edge=None):
    lane = lax.broadcasted_iota(jnp.int32, (8, LANES), 1)
    whole_row = lax.broadcasted_iota(jnp.int32, (8, LANES), 0)
    row = whole_row.astype(F32)
    last, first = lane == LANES - 1, lane == 0
    keep = weight * (1.0 - 4.0 * viscous * time_step)
    spread = weight * viscous * time_step
    half = -weight * time_step * 0.5
    turn = weight * time_step * coriolis

    def one(r, low_high=None):
        here, north, south = pl.ds(r, 8), pl.ds(r + 1, 8), pl.ds(r - 1, 8)
        there = pl.ds(r - shift, 8)
        if low_high is None:
            clip = lambda out: out
        else:
            at = whole_row + r
            valid = (at >= low_high[0]) & (at < low_high[1])
            clip = lambda out: jnp.where(valid, out, 0.0)
        lat = ((row + r.astype(F32)) * lat1 + lat0) * turn
        cells, rolls = {}, {}

        def cell(f, c):
            if (f, c) not in cells:
                cells[f, c] = src[f, c, here, :]
            return cells[f, c]

        def rolled(f, c, by):
            if (f, c, by) not in rolls:
                rolls[f, c, by] = pltpu.roll(cell(f, c), by, 1)
            return rolls[f, c, by]

        for c in range(CHUNKS):
            E, W, N, S, dx, dy, out = [], [], [], [], [], [], []
            for f in range(FIELDS):
                e = jnp.where(last, rolled(f, (c + 1) % CHUNKS, LANES - 1), rolled(f, c, LANES - 1))
                w = jnp.where(first, rolled(f, (c - 1) % CHUNKS, 1), rolled(f, c, 1))
                n, s = src[f, c, north, :], src[f, c, south, :]
                E.append(e)
                W.append(w)
                N.append(n)
                S.append(s)
                dx.append(e - w)
                dy.append(n - s)
                o = keep * cell(f, c) + spread * ((e + w) + (n + s))
                if base is not None:
                    o = o + old * base[f, c, here, :]
                out.append(o)
            u, v = cell(1, c), cell(2, c)
            us, vs = half * u, half * v
            flux = (E[0] * E[1] - W[0] * W[1]) + (N[0] * N[2] - S[0] * S[2]) + (dx[1] + dy[2])
            dst[0, c, there, :] = clip(out[0] + half * flux)
            dst[1, c, there, :] = clip(out[1] + (us * dx[1] + vs * dy[1]) + (lat * v + half * dx[0]))
            dst[2, c, there, :] = clip(out[2] + (us * dx[2] + vs * dy[2]) + (half * dy[0] - lat * u))
            dst[3, c, there, :] = clip(out[3] + (us * dx[3] + vs * dy[3]))

    groups = -(-rows // 8)

    def two(pair, carry):
        for group in (2 * pair, 2 * pair + 1):
            one(jnp.minimum(start + 8 * group, start + rows - 8))
        return carry

    if edge is not None:
        for group in range(groups):
            one(start + 8 * group, edge[1:] if group == edge[0] else None)
        return

    if groups > 1:
        lax.fori_loop(0, groups // 2, two, 0)
    if groups % 2:
        one(start + rows - 8)


def kernel(
    all_parents, state, perturbation, after, score,
    parents, A, C, Y, top, bottom, noise, acc, got, *rest,
):
    pieces = len(PIECES)
    H, V, X = (rest[i * pieces:(i + 1) * pieces] for i in range(3))
    (load_sem, halo_send, halo_recv, sum_send, sum_recv,
     y_send, y_recv, x_send, x_recv) = rest[3 * pieces:]
    m, d = lax.axis_index("member"), lax.axis_index("domain")
    y, xh, core = m // 4, (m // 2) % 2, m % 2
    xl, z = d // 8, d % 8
    rows = state.shape[2]
    domains = 16
    total_rows = rows * domains

    def member(y_, xh_, core_):
        return (y_ * 2 + xh_) * 2 + core_

    y_next, y_prev = (y + 1) % 4, (y + 3) % 4
    across = [(member(y, 1 - xh, k), d) for k in (0, 1)]
    other = (member(y, xh, 1 - core), d)
    d_next, d_prev = (m, (d + 1) % domains), (m, (d + domains - 1) % domains)

    x_side, z_next, z_prev = (m, (1 - xl) * 8 + z), (m, xl * 8 + (z + 1) % 8), (m, xl * 8 + (z + 7) % 8)
    z_next2, z_prev2 = (m, xl * 8 + (z + 2) % 8), (m, xl * 8 + (z + 6) % 8)

    greeted = [d_next, d_prev, z_next, z_prev, x_side, other] + across
    greeted += [(member(yy, xh, k), d) for yy in (y_next, y_prev) for k in (0, 1)]

    barrier = pltpu.get_barrier_semaphore()
    for device in greeted:
        pl.semaphore_signal(barrier, inc=1, device_id=device, device_id_type=MESH)

    loads = []
    for c in range(CHUNKS):
        lanes = pl.ds(c * LANES, LANES)
        loads.append(pltpu.make_async_copy(state.at[0, :, :, lanes], A.at[:, c, pl.ds(OWN, rows), :], load_sem.at[0, c]))
    for c in range(CHUNKS):
        lanes = pl.ds(c * LANES, LANES)
        loads.append(pltpu.make_async_copy(perturbation.at[0, :, :, lanes], noise.at[:, c, :, :], load_sem.at[1, c]))
    loads.append(pltpu.make_async_copy(all_parents, parents, load_sem.at[2, 0]))
    for load in loads:
        load.start()

    pl.semaphore_wait(barrier, len(greeted))

    def remote(src, dst, send, recv, device):
        copy = pltpu.make_async_remote_copy(
            src_ref=src, dst_ref=dst, send_sem=send, recv_sem=recv, device_id=device, device_id_type=MESH
        )
        copy.start()
        return copy

    def southward(B, which):
        return pltpu.make_async_remote_copy(
            src_ref=B.at[:, :, pl.ds(OWN, HALO), :], dst_ref=B.at[:, :, pl.ds(OWN + rows, HALO), :],
            send_sem=halo_send.at[which, 0], recv_sem=halo_recv.at[which, 0], device_id=d_prev, device_id_type=MESH)

    def northward(B, which):
        return pltpu.make_async_remote_copy(
            src_ref=B.at[:, :, pl.ds(OWN + rows - HALO, HALO), :], dst_ref=B.at[:, :, pl.ds(OWN - HALO, HALO), :],
            send_sem=halo_send.at[which, 1], recv_sem=halo_recv.at[which, 1], device_id=d_next, device_id_type=MESH)

    def at_south(act):
        pl.when(d > 0)(act)

    def at_north(act):
        pl.when(d < domains - 1)(act)

    first_row = (d * rows - OWN).astype(F32)
    nil = d // domains
    lat0 = 2.0 * (first_row + 0.5) / total_rows - 1.0
    lat1 = 2.0 / total_rows
    nothing = jnp.zeros((FIELDS, CHUNKS, 8, LANES), F32)

    def clear_south(B):
        @pl.when(d == 0)
        def _():
            B[:, :, pl.ds(OWN - 8, 8), :] = nothing

    def clear_north(B):
        @pl.when(d == domains - 1)
        def _():
            B[:, :, pl.ds(OWN + rows, 8), :] = nothing

    low = jnp.where(d == 0, OWN, 0)
    high = jnp.where(d == domains - 1, OWN + rows, BUFFER_ROWS)

    def run(B, first, count, k, dst=None, shift=0, edge=None):
        levels = [B] + [Y.at[i] for i in range(STAGES)]
        weight, old = ((1.0, 0.0), (0.25, 0.75), (2.0 / 3.0, 1.0 / 3.0))[(k - 1) % 3]
        base = levels[k - 1 - (k - 1) % 3] if old else None
        stage(levels[k - 1], base, dst if dst is not None else levels[k], OWN + first + nil, count, weight, old, lat0, lat1, shift, edge)

    def inside(B, until, stages):
        for k in stages:
            run(B, k, until - 2 * k, k)

    def south(B, result, shift):
        clear_south(B)
        for k in range(1, STAGES):
            run(B, k - STAGES, 16, k, edge=(0, low, BUFFER_ROWS))
        run(B, 0, 16, STAGES, result, shift)

    def north(B, wide, result, shift, meanwhile={}):
        clear_north(B)
        for k in range(1, STAGES):
            run(B, rows + STAGES - k - wide, wide, k, edge=(wide // 8 - 1, 0, high))
            if k in meanwhile:
                meanwhile[k]()
        run(B, rows - 16, 16, STAGES, result, shift)

    for load in loads[:CHUNKS]:
        load.wait()
    at_south(lambda: southward(A, 0).start())
    at_north(lambda: northward(A, 0).start())
    inside(A, rows, range(1, STAGES + 1))

    sums = []

    def weigh():
        row = lax.broadcasted_iota(jnp.int32, (8, LANES), 0).astype(F32)
        total = jnp.zeros((8, LANES), F32)
        for g in range(rows // 8):
            weight = 1.0 + 2.0 * (row + (d * rows + 8 * g).astype(F32)) / (total_rows - 1)
            squares = jnp.zeros((8, LANES), F32)
            for c in range(CHUNKS):
                q = (top, bottom)[g // 2][3, c, pl.ds(8 * (g % 2), 8), :]
                squares = squares + q * q
            total = total + weight * squares
        acc[0] = total

    def add_up():
        step = len(sums)
        for copy in sums[-1] if sums else ():
            copy.wait()
        if step == 0:
            sums.append([remote(acc.at[0], acc.at[1], sum_send.at[0, 0], sum_recv.at[0, 0], x_side)])
            return
        plan = ()
        if step == 1:
            got[z] = acc[0] + acc[1]
            plan = ((z_next, z), (z_prev, z))
        if step == 2:
            plan = ((z_next2, z), (z_prev2, z), (z_next2, (z + 7) % 8), (z_prev2, (z + 1) % 8))
        if step == 3:
            plan = ((z_prev2, (z + 2) % 8),)
        if plan:
            sums.append([remote(got.at[slot], got.at[slot], sum_send.at[step, way], sum_recv.at[step, way], device)
                         for way, (device, slot) in enumerate(plan)])

    mine, theirs = pl.ds(2 * core, 2), pl.ds(2 * (1 - core), 2)
    far = (y + 2) % 4
    sent, local = [], [None] * pieces

    def arrived(buffer, sem):
        pltpu.make_async_copy(buffer, buffer, sem).wait()

    def ring(i):
        A, begin = ((Y.at[STAGES - 1], OWN + PIECES[i][0]), (top, 0), (bottom, 16 - PIECES[i][1]))[i]
        part = pl.ds(begin, PIECES[i][1])
        place = H[i].at[y, core]
        for way, yy in enumerate((y_next, y_prev)):
            for k in (0, 1):
                sent.append(remote(A.at[pl.ds(2 * k, 2), :, part, :], place, y_send.at[i, 2 * way + k],
                                   y_recv.at[i, way, core], (member(yy, xh, k), d)))
        sent.append(remote(A.at[theirs, :, part, :], place, y_send.at[i, 4], y_recv.at[i, 2, 0], other))
        local[i] = pltpu.make_async_copy(A.at[mine, :, part, :], place, y_send.at[i, 7])
        local[i].start()

    def forward(i):
        for way, (block, yy) in enumerate(((H[i].at[y_prev, 0], y_next), (H[i].at[y_next, 1], y_prev))):
            arrived(block, y_recv.at[i, way, way])
            sent.append(remote(block, block, y_send.at[i, 5 + way], y_recv.at[i, 2, 1 + way], (member(yy, xh, core), d)))

    def choose(i):
        arrived(H[i].at[y_prev, 1], y_recv.at[i, 0, 1])
        arrived(H[i].at[y_next, 0], y_recv.at[i, 1, 0])
        arrived(H[i].at[y, 1 - core], y_recv.at[i, 2, 0])
        local[i].wait()
        arrived(H[i].at[far, 0], y_recv.at[i, 2, 1])
        arrived(H[i].at[far, 1], y_recv.at[i, 2, 2])
        for j, (home, device) in enumerate(((1 - xh, across[0]), (1 - xh, across[1]), (xh, other))):
            p = parents[member(y, home, (0, 1, 1 - core)[j])]
            V[i][j] = H[i][p // 4, p % 2]
            slot = 2 if j == 2 else core
            sent.append(remote(V[i].at[j], X[i].at[slot], x_send.at[i, j], x_recv.at[i, slot], device))

    def take(i):
        begin, count = PIECES[i]
        for slot in range(3):
            arrived(X[i].at[slot], x_recv.at[i, slot])
        p = parents[m]
        near = (p // 2) % 2 == xh
        into, add = pl.ds(OWN + begin, count), pl.ds(begin, count)
        C[mine, :, into, :] = noise[mine, :, add, :] + jnp.where(near, H[i][p // 4, p % 2], X[i][core])
        C[theirs, :, into, :] = noise[theirs, :, add, :] + jnp.where(near, X[i][2], X[i][1 - core])

    ring(MIDDLE)
    at_south(lambda: northward(A, 0).wait_recv())
    south(A, top, OWN)
    ring(TOP)
    at_north(lambda: southward(A, 0).wait_recv())
    north(A, 16, bottom, OWN + 16, {5: lambda: forward(MIDDLE)})
    ring(BOTTOM)
    forward(TOP)
    weigh()
    add_up()
    for load in loads[CHUNKS:]:
        load.wait()
    choose(MIDDLE)
    forward(BOTTOM)
    choose(TOP)
    choose(BOTTOM)
    add_up()
    take(MIDDLE)
    take(TOP)
    at_south(lambda: southward(C, 1).start())
    add_up()
    inside(C, PIECES[BOTTOM][0], range(1, STAGES))
    take(BOTTOM)
    at_north(lambda: northward(C, 1).start())
    add_up()

    class Result:
        def __setitem__(self, at, value):
            f, c, here, _ = at
            after[0, f, pl.ds(pl.multiple_of(here.start, 8), here.size), pl.ds(c * LANES, LANES)] = value

    at_north(lambda: southward(C, 1).wait_recv())
    north(C, 24, Result(), OWN)
    at_south(lambda: northward(C, 1).wait_recv())
    south(C, Result(), OWN)
    add_up()
    total = got[0]
    for other_z in range(1, 8):
        total = total + got[other_z]
    score[0] = jnp.sum(total) / (total_rows * state.shape[3])
    for copy in sent:
        copy.wait_send()
    for which, B in enumerate((A, C)):
        at_south(lambda: southward(B, which).wait_send())
        at_north(lambda: northward(B, which).wait_send())


def solution(mesh):
    def on_device(state, perturbation, parents):
        rows = state.shape[2]
        buffer = pltpu.VMEM((FIELDS, CHUNKS, BUFFER_ROWS, LANES), F32)

        def each(*lead):
            return [pltpu.VMEM((*lead, 2, CHUNKS, count, LANES), F32) for _, count in PIECES]

        n = len(PIECES)
        dma = pltpu.SemaphoreType.DMA
        return pl.pallas_call(
            kernel,
            out_shape=(pltpu.VMEM(state.shape, F32), jax.ShapeDtypeStruct((1,), F32)),
            in_specs=[
                pl.BlockSpec(memory_space=pl.ANY),
                pl.BlockSpec(memory_space=pl.ANY),
                pl.BlockSpec(memory_space=pl.ANY),
            ],
            out_specs=(pl.BlockSpec(memory_space=pltpu.VMEM), pl.BlockSpec(memory_space=pltpu.SMEM)),
            scratch_shapes=[pltpu.SMEM(parents.shape, jnp.int32)]
            + [buffer] * 2
            + [pltpu.VMEM((STAGES, FIELDS, CHUNKS, BUFFER_ROWS, LANES), F32)]
            + [pltpu.VMEM((FIELDS, CHUNKS, 16, LANES), F32)] * 2
            + [pltpu.VMEM((FIELDS, CHUNKS, rows, LANES), F32)]
            + [pltpu.VMEM((2, 8, LANES), F32), pltpu.VMEM((8, 8, LANES), F32)]
            + each(4, 2) + each(3) + each(3)
            + [dma((3, 4)), dma((2, 2)), dma((2, 2)), dma((4, 4)), dma((4, 4)),
               dma((n, 8)), dma((n, 3, 3)), dma((n, 3)), dma((n, 3))],
            compiler_params=pltpu.CompilerParams(collective_id=0, has_side_effects=True),
        )(parents, state, perturbation)

    placed = P("member", None, "domain", None)
    return jax.shard_map(
        on_device, mesh=mesh, in_specs=(placed, placed, P()), out_specs=(placed, P("member")), check_vma=False
    )
```
